32 devices in a mesh: freq: 16 (over z, x, core), rcv: 2 (over y).
Axes of the slice: x: 2, y: 2, z: 4, core: 2. Of those that a mesh axis runs over, the one named last changes fastest.
Arguments:
- reflection: bfloat16 [2, 128, 768, 768], P(None, 'freq', 'rcv'), may hold values from -0.21875 to 0.21875
- direct: bfloat16 [768, 128, 512], P(('rcv', 'freq')), may hold values from -6 to 6
- onset: int32 [768, 128], P(('rcv', 'freq')), may hold values from 128 to 383
Outputs:
- focus_plus: bfloat16 [768, 128, 512], P(('rcv', 'freq'))
- focus_minus: bfloat16 [768, 128, 512], P(('rcv', 'freq'))
- correlation: float32 [2, 128, 128, 128], P(None, 'freq', 'rcv')
The draws below stay inside these ranges and needn't reach their ends.
All inputs are finite; a program needn't handle non-finite values.
Results may differ from the reference program's by a relative error of at most 0.019.
Values may be sent and summed in bfloat16 or wider, within the bound.
A program may use at most 64 MiB of HBM per device.

```python
import math
import jax
import jax.numpy as jnp
from jax import lax

NS = 768
NF = 128
NT = 512
NFOC = 128
ITERS = 1
SRC_BLOCK = 384


def with_ends(values, own_key, low, high):
    index_at = [jax.random.randint(jax.random.fold_in(own_key, axis), (), 0, length) for axis, length in enumerate(values.shape)]
    main_axis = values.shape.index(max(values.shape))
    beside = index_at[:main_axis] + [(index_at[main_axis] + 1) % values.shape[main_axis]] + index_at[main_axis + 1:]
    return values.at[tuple(index_at)].set(low).at[tuple(beside)].set(high)


def shard_levels(rng, dims, split, least, largest):
    level = 1.0
    for dim, shards_of in split:
        draws = jax.random.uniform(jax.random.fold_in(jax.random.fold_in(rng, 6), dim), (shards_of,), jnp.float32, least / len(split), largest / len(split))
        level = level * jnp.repeat(jnp.exp(draws), dims[dim] // shards_of).reshape((-1,) + (1,) * (len(dims) - 1 - dim))
    return level


def bell_draw(stream_key, dims, spread, reach, split=(), held_as=jnp.bfloat16):
    entries = spread * jax.random.normal(stream_key, dims, jnp.float32)
    if split:
        entries = entries * shard_levels(stream_key, dims, split, -0.22, 0.18)
    return jnp.clip(entries, -reach, reach).astype(held_as)


def setup_inputs(seed: int = 0) -> dict:
    seeds = jax.random.split(jax.random.key(seed), 4)
    return {
        "reflection": bell_draw(seeds[0], (2, NF, NS, NS), NS ** -0.5, 0.21875, ((1, 16), (2, 2))),
        "direct": bell_draw(seeds[1], (NS, NFOC, NT), 1.0, 6.0, ((0, 32),)),
        "onset": with_ends(jax.random.randint(seeds[2], (NS, NFOC), NT // 4, 3 * NT // 4), jax.random.fold_in(seeds[2], 1), NT // 4, (3 * NT // 4) - 1).astype(jnp.int32),
    }


def lookup_tables():
    sample = jnp.arange(NT, dtype=jnp.int32)
    spectral_bin_index = jnp.arange(NF, dtype=jnp.int32)
    phase_index = sample[:, None] * spectral_bin_index[None, :] % NT
    angles = 2.0 * math.pi / NT * phase_index.astype(jnp.float32)
    cosine = jnp.cos(angles)
    sine = jnp.sin(angles)
    forward = (jnp.stack([cosine, -sine], axis=1) / math.sqrt(NT)).astype(jnp.bfloat16)
    inverse = (jnp.stack([cosine.T, -sine.T], axis=0) * (2.0 / math.sqrt(NT))).astype(jnp.bfloat16)
    return (forward, inverse)

def fourier_spectrum(field, forward):
    result = jnp.einsum('sqt,tcf->scfq', field.astype(jnp.float32), forward.astype(jnp.float32))
    return result.astype(jnp.bfloat16)

def apply_reflection(spectra, reflection, conj_sign):
    block_count = NS // SRC_BLOCK
    refl_blocks = reflection.reshape(2, NF, block_count, SRC_BLOCK, NS).transpose(2, 0, 1, 3, 4)
    spec_blocks = spectra.reshape(block_count, SRC_BLOCK, 2, NF, NFOC)

    def accumulate(summed, blocks):
        refl_block, spec_block = blocks
        refl_real = refl_block[0].astype(jnp.float32)
        refl_imag = refl_block[1].astype(jnp.float32)
        spectrum_real_rows = spec_block[:, 0].astype(jnp.float32)
        spec_imag = spec_block[:, 1].astype(jnp.float32)

        def product(left_operand, right_operand):
            return jnp.einsum('key,ekn->ykn', left_operand, right_operand)
        real_part = product(refl_real, spectrum_real_rows) - conj_sign * product(refl_imag, spec_imag)
        imag_part = product(refl_real, spec_imag) + conj_sign * product(refl_imag, spectrum_real_rows)
        rounded = jnp.stack([real_part, imag_part], axis=1).astype(jnp.bfloat16)
        rounded = lax.optimization_barrier(rounded)
        return (summed + rounded.astype(jnp.float32), None)
    start = jnp.zeros((NS, 2, NF, NFOC), jnp.float32)
    summed, _ = lax.scan(accumulate, start, (refl_blocks, spec_blocks))
    return summed

def inverse_window(summed, onset, inverse):
    traces = jnp.einsum('scfq,cft->sqt', summed.astype(jnp.float32), inverse.astype(jnp.float32))
    sample = jnp.arange(NT, dtype=jnp.int32)
    window = (sample[None, None, :] < onset[:, :, None]).astype(jnp.float32)
    return traces * window

def reference(reflection, direct, onset):
    forward, inverse = lookup_tables()
    focus_plus = direct
    focus_minus = direct
    minus_spectrum = fourier_spectrum(direct, forward)
    for sweep in range(ITERS):
        plus_spectrum = fourier_spectrum(focus_plus, forward)
        summed = apply_reflection(plus_spectrum, reflection, 1.0).astype(jnp.bfloat16)
        focus_minus = inverse_window(summed, onset, inverse).astype(jnp.bfloat16)
        minus_spectrum = fourier_spectrum(focus_minus, forward)
        summed = apply_reflection(minus_spectrum, reflection, -1.0).astype(jnp.bfloat16)
        focus_plus = (direct.astype(jnp.float32) + inverse_window(summed, onset, inverse)).astype(jnp.bfloat16)
    plus_spectrum = fourier_spectrum(focus_plus, forward)
    green_field = (apply_reflection(plus_spectrum, reflection, 1.0) - minus_spectrum.astype(jnp.float32)).astype(jnp.bfloat16)
    green_real = green_field[:, 0].astype(jnp.float32)
    green_imag = green_field[:, 1].astype(jnp.float32)
    real_part = jnp.einsum('rfa,rfb->fab', green_real, green_real) + jnp.einsum('rfa,rfb->fab', green_imag, green_imag)
    imag_part = jnp.einsum('rfa,rfb->fab', green_real, green_imag) - jnp.einsum('rfa,rfb->fab', green_imag, green_real)
    correlation = jnp.stack([real_part, imag_part], axis=0) / NS
    return (focus_plus, focus_minus, correlation)
```

```python
import math

import jax
import jax.numpy as jnp
from jax import lax
from jax.sharding import PartitionSpec as P

CHUNKS = 2


def lookup_tables(samples, frequencies):
    sample = jnp.arange(samples, dtype=jnp.int32)
    spectral_bin_index = jnp.arange(frequencies, dtype=jnp.int32)
    phase_index = sample[:, None] * spectral_bin_index[None, :] % samples
    angles = 2.0 * math.pi / samples * phase_index.astype(jnp.float32)
    cosine = jnp.cos(angles)
    sine = jnp.sin(angles)
    forward = (jnp.stack([cosine, -sine], axis=1) / math.sqrt(samples)).astype(jnp.bfloat16)
    inverse = (jnp.stack([cosine.T, -sine.T], axis=0) * (2.0 / math.sqrt(samples))).astype(
        jnp.bfloat16
    )
    return (forward, inverse)


def spectrum_of(field, forward):
    local = jnp.einsum(
        "sqt,tcf->sfcq", field, forward, preferred_element_type=jnp.float32
    ).astype(jnp.bfloat16)
    return local.reshape(local.shape[0], local.shape[1], -1)


def to_frequencies(local):
    return lax.all_to_all(local, "freq", split_axis=1, concat_axis=0, tiled=True)


def partial_product(spectra, reflection, sign):
    half = spectra.shape[2] // 2
    real = spectra[:, :, :half]
    imag = spectra[:, :, half:]
    turned = jnp.concatenate([-imag, real] if sign > 0 else [imag, -real], axis=2)
    operand = jnp.stack([spectra, turned], axis=0)
    return jnp.einsum(
        "cfsr,csfn->rfn", reflection, operand, preferred_element_type=jnp.float32
    ).astype(jnp.bfloat16)


def sum_blocks(partial):
    return lax.psum_scatter(partial, "rcv", scatter_dimension=0, tiled=True)


def to_traces(summed):
    return lax.all_to_all(summed, "freq", split_axis=0, concat_axis=1, tiled=True)


def inverse_window(summed, onset, inverse):
    spectra = summed.reshape(summed.shape[0], summed.shape[1], 2, -1)
    traces = jnp.einsum("sfcq,cft->sqt", spectra, inverse, preferred_element_type=jnp.float32)
    sample = jnp.arange(traces.shape[2], dtype=jnp.int32)
    window = (sample[None, None, :] < onset[:, :, None]).astype(jnp.float32)
    return traces * window


def on_device(reflection, direct, onset):
    samples = direct.shape[2]
    frequencies = reflection.shape[1] * lax.axis_size("freq")
    receivers = reflection.shape[3]
    forward, inverse = lookup_tables(samples, frequencies)
    width = direct.shape[1] // CHUNKS
    plus_out, minus_out, green_out = [], [], []
    for chunk in range(CHUNKS):
        part = slice(chunk * width, (chunk + 1) * width)
        field, edge = direct[:, part], onset[:, part]
        spectra = to_frequencies(spectrum_of(field, forward))
        back = to_traces(sum_blocks(partial_product(spectra, reflection, 1)))
        minus = inverse_window(back, edge, inverse).astype(jnp.bfloat16)
        minus_spectrum = to_frequencies(spectrum_of(minus, forward))
        back = to_traces(sum_blocks(partial_product(minus_spectrum, reflection, -1)))
        plus = (field.astype(jnp.float32) + inverse_window(back, edge, inverse)).astype(
            jnp.bfloat16
        )
        spectra = to_frequencies(spectrum_of(plus, forward))
        summed = sum_blocks(partial_product(spectra, reflection, 1)).astype(jnp.float32)
        green = (summed - minus_spectrum.astype(jnp.float32)).astype(jnp.bfloat16)
        plus_out.append(plus)
        minus_out.append(minus)
        green_out.append(green.reshape(green.shape[0], green.shape[1], 2, width))
    green = jnp.concatenate(green_out, axis=3)
    green_real = green[:, :, 0]
    green_imag = green[:, :, 1]

    def pairwise(left_operand, right_operand):
        return jnp.einsum(
            "rfa,rfb->fab", left_operand, right_operand, preferred_element_type=jnp.float32
        )

    real_part = pairwise(green_real, green_real) + pairwise(green_imag, green_imag)
    imag_part = pairwise(green_real, green_imag) - pairwise(green_imag, green_real)
    partial_corr = jnp.stack([real_part, imag_part], axis=0) / receivers
    correlation = lax.psum_scatter(
        partial_corr.astype(jnp.bfloat16), "rcv", scatter_dimension=2, tiled=True
    ).astype(jnp.float32)
    return (
        jnp.concatenate(plus_out, axis=1),
        jnp.concatenate(minus_out, axis=1),
        correlation,
    )


def solution(mesh):
    placed = (
        P(None, "freq", "rcv", None),
        P(("rcv", "freq"), None, None),
        P(("rcv", "freq"), None),
    )
    return jax.shard_map(
        on_device,
        mesh=mesh,
        in_specs=placed,
        out_specs=(
            P(("rcv", "freq"), None, None),
            P(("rcv", "freq"), None, None),
            P(None, "freq", "rcv", None),
        ),
        check_vma=False,
    )
```

```python
import functools
import math

import jax
import jax.numpy as jnp
from jax import lax
from jax.experimental import pallas as pl
from jax.experimental.pallas import tpu as pltpu
from jax.sharding import PartitionSpec as P


def lookup_tables(samples, frequencies):
    sample = jnp.arange(samples, dtype=jnp.int32)
    spectral_bin_index = jnp.arange(frequencies, dtype=jnp.int32)
    phase_index = sample[:, None] * spectral_bin_index[None, :] % samples
    angles = 2.0 * math.pi / samples * phase_index.astype(jnp.float32)
    cosine = jnp.cos(angles)
    sine = jnp.sin(angles)
    forward = (jnp.stack([cosine, -sine], axis=1) / math.sqrt(samples)).astype(jnp.bfloat16)
    inverse = (jnp.stack([cosine.T, -sine.T], axis=0) * (2.0 / math.sqrt(samples))).astype(
        jnp.bfloat16
    )
    return (forward, inverse)


def fourier_spectrum(field, forward):
    local_spectra = jnp.einsum(
        "sqt,tcf->scfq", field, forward, preferred_element_type=jnp.float32
    ).astype(jnp.bfloat16)
    return lax.all_to_all(local_spectra, "freq", split_axis=2, concat_axis=0, tiled=True)


def make_term(spectra, reflection, conj_sign):
    spectrum_real_rows = spectra[:, 0]
    spec_imag = spectra[:, 1]

    def product(left_operand, right_operand):
        return jnp.einsum(
            "key,ekn->ykn", left_operand, right_operand, preferred_element_type=jnp.float32
        )

    real_part = product(reflection[0], spectrum_real_rows) - conj_sign * product(
        reflection[1], spec_imag
    )
    imag_part = product(reflection[0], spec_imag) + conj_sign * product(
        reflection[1], spectrum_real_rows
    )
    return jnp.stack([real_part, imag_part], axis=1)


def to_time(spectra, reflection, conj_sign):
    summed = lax.psum_scatter(
        make_term(spectra, reflection, conj_sign).astype(jnp.bfloat16),
        "rcv",
        scatter_dimension=0,
        tiled=True,
    )
    return lax.all_to_all(summed, "freq", split_axis=0, concat_axis=2, tiled=True)


def inverse_window(summed, onset, inverse):
    traces = jnp.einsum("scfq,cft->sqt", summed, inverse, preferred_element_type=jnp.float32)
    sample = jnp.arange(traces.shape[2], dtype=jnp.int32)
    window = (sample[None, None, :] < onset[:, :, None]).astype(jnp.float32)
    return traces * window


def on_device(reflection, direct, onset):
    samples = direct.shape[2]
    frequencies = reflection.shape[1] * lax.axis_size("freq")
    forward, inverse = lookup_tables(samples, frequencies)
    focus_plus = direct
    minus_spectrum = None
    plus_spectrum = fourier_spectrum(focus_plus, forward)
    focus_minus = inverse_window(to_time(plus_spectrum, reflection, 1.0), onset, inverse).astype(
        jnp.bfloat16
    )
    minus_spectrum = fourier_spectrum(focus_minus, forward)
    returned = inverse_window(to_time(minus_spectrum, reflection, -1.0), onset, inverse)
    focus_plus = (direct.astype(jnp.float32) + returned).astype(jnp.bfloat16)
    plus_spectrum = fourier_spectrum(focus_plus, forward)
    receivers = reflection.shape[3]
    summed = lax.psum_scatter(
        make_term(plus_spectrum, reflection, 1.0).astype(jnp.bfloat16),
        "rcv",
        scatter_dimension=0,
        tiled=True,
    ).astype(jnp.float32)
    green_field = (summed - minus_spectrum.astype(jnp.float32)).astype(jnp.bfloat16)
    green_real = green_field[:, 0]
    green_imag = green_field[:, 1]

    def pairwise(left_operand, right_operand):
        return jnp.einsum(
            "rfa,rfb->fab", left_operand, right_operand, preferred_element_type=jnp.float32
        )

    real_part = pairwise(green_real, green_real) + pairwise(green_imag, green_imag)
    imag_part = pairwise(green_real, green_imag) - pairwise(green_imag, green_real)
    partial_corr = jnp.stack([real_part, imag_part], axis=0) / receivers
    correlation = lax.psum_scatter(
        partial_corr.astype(jnp.bfloat16), "rcv", scatter_dimension=2, tiled=True
    ).astype(jnp.float32)
    return (focus_plus, focus_minus, correlation)


CHUNKS = 2
GROUP = 4
MESH = pl.DeviceIdType.MESH


def kernel(
    n, direct, onset, fwd, inv, refl, fp, fm, corr,
    ref_t, stage, zs, zr, ys, yr, rs, rr, own, minus, green, rows, cs, cr,
    load_sem, z_send, z_recv, y_send, y_recv, r_send, r_recv, c_send, c_recv,
):
    me = lax.axis_index("freq")
    side = lax.axis_index("rcv")
    other = 1 - side
    traces, points, samples = direct.shape
    width = points // CHUNKS
    lanes = 2 * width
    bins, receivers, _ = ref_t.shape
    sources = receivers // 2
    freqs = n * bins
    groups = traces // GROUP
    f32, bf16 = jnp.float32, jnp.bfloat16

    barrier = pltpu.get_barrier_semaphore()

    def greet(k, carry):
        pl.semaphore_signal(
            barrier, inc=1, device_id=(lax.rem(me + k, n), side), device_id_type=MESH
        )
        return carry

    lax.fori_loop(1, n, greet, 0)
    pl.semaphore_signal(barrier, inc=1, device_id=(me, other), device_id_type=MESH)

    def load(f):
        slot = lax.rem(f, 2)
        return pltpu.make_async_copy(refl.at[:, f], stage.at[slot], load_sem.at[slot])

    load(0).start()
    load(1).start()

    def exchange(src, dst, send, recv, k):
        o = n // 2 + k
        off = o - (n - 1) * (o // n)
        peer = lax.rem(me + off, n)
        return pltpu.make_async_remote_copy(
            src_ref=src.at[peer],
            dst_ref=dst.at[me],
            send_sem=send.at[off],
            recv_sem=recv.at[off],
            device_id=(peer, side),
            device_id_type=MESH,
        )

    def arrival(src, dst, send, recv, off):
        giver = lax.rem(me - off + n, n)
        return pltpu.make_async_remote_copy(
            src_ref=src.at[giver],
            dst_ref=dst.at[giver],
            send_sem=send.at[off],
            recv_sem=recv.at[off],
            device_id=(giver, side),
            device_id_type=MESH,
        )

    def send_all(ops):
        def step(k, carry):
            exchange(*ops, k).start()
            return carry

        lax.fori_loop(0, n - 1, step, 0)
        src, dst = ops[0], ops[1]
        dst[me] = src[me]

    def wait_all(ops):
        def step(off, carry):
            arrival(*ops, off).wait_recv()
            return carry

        lax.fori_loop(1, n, step, 0)

    def drain_all(ops):
        def step(off, carry):
            arrival(*ops, off).wait_send()
            return carry

        lax.fori_loop(1, n, step, 0)

    def z_ops(p, c):
        return zs.at[p, c], zr.at[p, c], z_send.at[p, c], z_recv.at[p, c]

    def y_ops(p, c):
        return ys.at[p, c], yr.at[p, c], y_send.at[p, c], y_recv.at[p, c]

    def half_copy(p, c, f):
        return pltpu.make_async_remote_copy(
            src_ref=rs.at[p, c, f],
            dst_ref=rr.at[p, c, f],
            send_sem=r_send.at[p, c, f],
            recv_sem=r_recv.at[p, c, f],
            device_id=(me, other),
            device_id_type=MESH,
        )

    def corr_copy(f):
        return pltpu.make_async_remote_copy(
            src_ref=cs.at[other, f],
            dst_ref=cr.at[f],
            send_sem=c_send.at[f],
            recv_sem=c_recv.at[f],
            device_id=(me, other),
            device_id_type=MESH,
        )

    def to_spectrum(p, c, g, block):
        spec = jnp.dot(block, fwd[...], preferred_element_type=f32)
        for u in range(GROUP):
            a = spec[u * width : (u + 1) * width]
            turned = jnp.concatenate([a[:, :freqs], a[:, freqs:]], axis=0).T
            zs[p, c, :, g * GROUP + u] = turned.reshape(n, bins, lanes).astype(bf16)

    def first(c):
        def step(g, carry):
            block = direct[pl.ds(g * GROUP, GROUP), c * width : (c + 1) * width, :]
            to_spectrum(0, c, g, block.reshape(GROUP * width, samples))
            return carry

        lax.fori_loop(0, groups, step, 0)

    def unpack(src):
        size = traces * bins

        def step(j, carry):
            rows[pl.ds(pl.multiple_of(j * size, size), size), :] = (
                src[j].astype(f32).reshape(size, lanes)
            )
            return carry

        lax.fori_loop(0, n, step, 0)

    def back(p, c):
        wait_all(y_ops(p, c))
        unpack(yr.at[p, c])
        cols = slice(c * width, (c + 1) * width)

        def step(g, carry):
            parts = []
            for u in range(GROUP):
                t = rows[pl.ds(g * GROUP + u, freqs, stride=traces), :].T
                parts.append(jnp.concatenate([t[:width], t[width:]], axis=1))
            lhs = jnp.concatenate(parts, axis=0).astype(bf16)
            out = jnp.dot(lhs, inv[...], preferred_element_type=f32)
            size = GROUP * width
            edge = onset[c, pl.ds(pl.multiple_of(g * size, size), size), :]
            sample = lax.broadcasted_iota(jnp.int32, out.shape, 1)
            out = jnp.where(sample < edge, out, 0.0)
            at = pl.ds(g * GROUP, GROUP)
            if p == 0:
                block = out.astype(bf16)
                fm[at, cols, :] = block.reshape(GROUP, width, samples)
            else:
                old = direct[at, cols, :].astype(f32).reshape(size, samples)
                block = (old + out).astype(bf16)
                fp[at, cols, :] = block.reshape(GROUP, width, samples)
            to_spectrum(p + 1, c, g, block)
            return carry

        lax.fori_loop(0, groups, step, 0)
        send_all(z_ops(p + 1, c))

    def apply(p, c, sign):
        wait_all(z_ops(p, c))
        unpack(zr.at[p, c])

        def step(f, carry):
            x = rows[pl.ds(f, sources, stride=bins), :]
            if p == 1:
                minus[c, f] = x.astype(bf16)
            y = pltpu.roll(x, width, 1)
            low = lax.broadcasted_iota(jnp.int32, x.shape, 1) < width
            y = jnp.where(low, -y, y) if sign > 0 else jnp.where(low, y, -y)
            w = jnp.concatenate([x.astype(bf16), y.astype(bf16)], axis=0)
            theirs = ref_t[f, pl.ds(pl.multiple_of(other * sources, sources), sources), :]
            rs[p, c, f] = jnp.dot(theirs, w, preferred_element_type=f32).astype(bf16)
            half_copy(p, c, f).start()
            mine = ref_t[f, pl.ds(pl.multiple_of(side * sources, sources), sources), :]
            own[c, f] = jnp.dot(mine, w, preferred_element_type=f32).astype(bf16)
            return carry

        lax.fori_loop(0, bins, step, 0)

    def reduce(p, c):
        def step(f, carry):
            half_copy(p, c, f).wait_recv()
            total = own[c, f].astype(f32) + rr[p, c, f].astype(f32)
            if p < 2:
                ys[p, c, :, f] = total.reshape(n, traces, lanes).astype(bf16)
            else:
                green[c, f] = (total - minus[c, f].astype(f32)).astype(bf16)
            return carry

        lax.fori_loop(0, bins, step, 0)
        if p < 2:
            send_all(y_ops(p, c))

    def transpose(f, carry):
        load(f).wait()
        slot = lax.rem(f, 2)
        for c in range(2):
            ref_t[f, :, c * sources : (c + 1) * sources] = stage[slot, c].T

        @pl.when(f + 2 < bins)
        def _():
            load(f + 2).start()

        return carry

    first(0)
    pl.semaphore_wait(barrier, n)
    send_all(z_ops(0, 0))
    first(1)
    send_all(z_ops(0, 1))
    lax.fori_loop(0, bins, transpose, 0)
    apply(0, 0, 1)
    reduce(0, 0)
    apply(0, 1, 1)
    reduce(0, 1)
    back(0, 0)
    back(0, 1)
    apply(1, 0, -1)
    reduce(1, 0)
    apply(1, 1, -1)
    reduce(1, 1)
    back(1, 0)
    back(1, 1)
    apply(2, 0, 1)
    reduce(2, 0)
    apply(2, 1, 1)
    reduce(2, 1)

    half = points // 2

    def correlate(f, carry):
        a, b = green[0, f].astype(f32), green[1, f].astype(f32)
        low = lax.broadcasted_iota(jnp.int32, a.shape, 1) < width
        real = jnp.where(low, a, pltpu.roll(b, width, 1))
        imag = jnp.where(low, pltpu.roll(a, width, 1), b)
        both = jnp.concatenate([real, imag], axis=1).astype(bf16)
        prod = lax.dot_general(
            both, both, (((0,), (0,)), ((), ())), preferred_element_type=f32
        )
        re = (prod[:points, :points] + prod[points:, points:]) / receivers
        im = (prod[:points, points:] - prod[points:, :points]) / receivers
        for h in range(2):
            cs[h, f, 0] = re[h * half : (h + 1) * half].astype(bf16)
            cs[h, f, 1] = im[h * half : (h + 1) * half].astype(bf16)
        corr_copy(f).start()
        return carry

    lax.fori_loop(0, bins, correlate, 0)

    def collect(f, carry):
        corr_copy(f).wait_recv()
        for c in range(2):
            corr[c, f] = cs[side, f, c].astype(f32) + cr[f, c].astype(f32)
        return carry

    lax.fori_loop(0, bins, collect, 0)

    for c in range(CHUNKS):
        for p in range(3):
            drain_all(z_ops(p, c))

            def drain(f, carry):
                half_copy(p, c, f).wait_send()
                return carry

            lax.fori_loop(0, bins, drain, 0)
        for p in range(2):
            drain_all(y_ops(p, c))

    def drain_corr(f, carry):
        corr_copy(f).wait_send()
        return carry

    lax.fori_loop(0, bins, drain_corr, 0)


def fused(reflection, direct, onset):
    n = lax.axis_size("freq")
    traces, points, samples = direct.shape
    _, bins, sources, receivers = reflection.shape
    width = points // CHUNKS
    frequencies = bins * n
    forward, inverse = lookup_tables(samples, frequencies)
    forward = forward.reshape(samples, 2 * frequencies)
    inverse = inverse.reshape(2 * frequencies, samples)
    edges = onset.reshape(traces, CHUNKS, width).transpose(1, 0, 2)
    edges = edges.reshape(CHUNKS, traces * width, 1)
    bf16, dma = jnp.bfloat16, pltpu.SemaphoreType.DMA
    lanes = 2 * width
    vmem = pl.BlockSpec(memory_space=pltpu.VMEM)
    return pl.pallas_call(
        functools.partial(kernel, n),
        out_shape=(
            jax.ShapeDtypeStruct(direct.shape, bf16),
            jax.ShapeDtypeStruct(direct.shape, bf16),
            jax.ShapeDtypeStruct((2, bins, points // 2, points), jnp.float32),
        ),
        in_specs=[vmem, vmem, vmem, vmem, pl.BlockSpec(memory_space=pl.ANY)],
        out_specs=(vmem, vmem, vmem),
        scratch_shapes=[
            pltpu.VMEM((bins, receivers, 2 * sources), bf16),
            pltpu.VMEM((2, 2, sources, receivers), bf16),
            pltpu.VMEM((3, CHUNKS, n, traces, bins, lanes), bf16),
            pltpu.VMEM((3, CHUNKS, n, traces, bins, lanes), bf16),
            pltpu.VMEM((2, CHUNKS, n, bins, traces, lanes), bf16),
            pltpu.VMEM((2, CHUNKS, n, bins, traces, lanes), bf16),
            pltpu.VMEM((3, CHUNKS, bins, sources, lanes), bf16),
            pltpu.VMEM((3, CHUNKS, bins, sources, lanes), bf16),
            pltpu.VMEM((CHUNKS, bins, sources, lanes), bf16),
            pltpu.VMEM((CHUNKS, bins, sources, lanes), bf16),
            pltpu.VMEM((CHUNKS, bins, sources, lanes), bf16),
            pltpu.VMEM((n * traces * bins, lanes), jnp.float32),
            pltpu.VMEM((2, bins, 2, points // 2, points), bf16),
            pltpu.VMEM((bins, 2, points // 2, points), bf16),
            dma((2,)),
            dma((3, CHUNKS, n)),
            dma((3, CHUNKS, n)),
            dma((2, CHUNKS, n)),
            dma((2, CHUNKS, n)),
            dma((3, CHUNKS, bins)),
            dma((3, CHUNKS, bins)),
            dma((bins,)),
            dma((bins,)),
        ],
        compiler_params=pltpu.CompilerParams(
            collective_id=0, has_side_effects=True, vmem_limit_bytes=67043328
        ),
    )(direct, edges, forward, inverse, reflection)


def fits(reflection, direct):
    n = lax.axis_size("freq")
    traces, points, samples = direct.shape
    _, bins, sources, receivers = reflection.shape
    return (
        lax.axis_size("rcv") == 2
        and receivers == 2 * sources
        and sources == n * traces
        and traces % 8 == 0
        and bins % 8 == 0
        and points == 128
        and samples % 128 == 0
        and (bins * n) % 128 == 0
    )


def per_device(reflection, direct, onset):
    if fits(reflection, direct):
        return fused(reflection, direct, onset)
    return on_device(reflection, direct, onset)


def solution(mesh):
    placed = (
        P(None, "freq", "rcv", None),
        P(("rcv", "freq"), None, None),
        P(("rcv", "freq"), None),
    )
    return jax.shard_map(
        per_device,
        mesh=mesh,
        in_specs=placed,
        out_specs=(
            P(("rcv", "freq"), None, None),
            P(("rcv", "freq"), None, None),
            P(None, "freq", "rcv", None),
        ),
        check_vma=False,
    )
```

```python
import functools
import math

import jax
import jax.numpy as jnp
import numpy as np
from jax import lax
from jax.experimental import pallas as pl
from jax.experimental.pallas import tpu as pltpu
from jax.sharding import PartitionSpec as P


def lookup_tables(samples, frequencies):
    sample = jnp.arange(samples, dtype=jnp.int32)
    spectral_bin_index = jnp.arange(frequencies, dtype=jnp.int32)
    phase_index = sample[:, None] * spectral_bin_index[None, :] % samples
    angles = 2.0 * math.pi / samples * phase_index.astype(jnp.float32)
    cosine = jnp.cos(angles)
    sine = jnp.sin(angles)
    forward = (jnp.stack([cosine, -sine], axis=1) / math.sqrt(samples)).astype(jnp.bfloat16)
    inverse = (jnp.stack([cosine.T, -sine.T], axis=0) * (2.0 / math.sqrt(samples))).astype(
        jnp.bfloat16
    )
    return (forward, inverse)


def fourier_spectrum(field, forward):
    local_spectra = jnp.einsum(
        "sqt,tcf->scfq", field, forward, preferred_element_type=jnp.float32
    ).astype(jnp.bfloat16)
    return lax.all_to_all(local_spectra, "freq", split_axis=2, concat_axis=0, tiled=True)


def make_term(spectra, reflection, conj_sign):
    spectrum_real_rows = spectra[:, 0]
    spec_imag = spectra[:, 1]

    def product(left_operand, right_operand):
        return jnp.einsum(
            "key,ekn->ykn", left_operand, right_operand, preferred_element_type=jnp.float32
        )

    real_part = product(reflection[0], spectrum_real_rows) - conj_sign * product(
        reflection[1], spec_imag
    )
    imag_part = product(reflection[0], spec_imag) + conj_sign * product(
        reflection[1], spectrum_real_rows
    )
    return jnp.stack([real_part, imag_part], axis=1)


def to_time(spectra, reflection, conj_sign):
    summed = lax.psum_scatter(
        make_term(spectra, reflection, conj_sign).astype(jnp.bfloat16),
        "rcv",
        scatter_dimension=0,
        tiled=True,
    )
    return lax.all_to_all(summed, "freq", split_axis=0, concat_axis=2, tiled=True)


def inverse_window(summed, onset, inverse):
    traces = jnp.einsum("scfq,cft->sqt", summed, inverse, preferred_element_type=jnp.float32)
    sample = jnp.arange(traces.shape[2], dtype=jnp.int32)
    window = (sample[None, None, :] < onset[:, :, None]).astype(jnp.float32)
    return traces * window


def on_device(reflection, direct, onset):
    samples = direct.shape[2]
    frequencies = reflection.shape[1] * lax.axis_size("freq")
    forward, inverse = lookup_tables(samples, frequencies)
    focus_plus = direct
    minus_spectrum = None
    plus_spectrum = fourier_spectrum(focus_plus, forward)
    focus_minus = inverse_window(to_time(plus_spectrum, reflection, 1.0), onset, inverse).astype(
        jnp.bfloat16
    )
    minus_spectrum = fourier_spectrum(focus_minus, forward)
    returned = inverse_window(to_time(minus_spectrum, reflection, -1.0), onset, inverse)
    focus_plus = (direct.astype(jnp.float32) + returned).astype(jnp.bfloat16)
    plus_spectrum = fourier_spectrum(focus_plus, forward)
    receivers = reflection.shape[3]
    summed = lax.psum_scatter(
        make_term(plus_spectrum, reflection, 1.0).astype(jnp.bfloat16),
        "rcv",
        scatter_dimension=0,
        tiled=True,
    ).astype(jnp.float32)
    green_field = (summed - minus_spectrum.astype(jnp.float32)).astype(jnp.bfloat16)
    green_real = green_field[:, 0]
    green_imag = green_field[:, 1]

    def pairwise(left_operand, right_operand):
        return jnp.einsum(
            "rfa,rfb->fab", left_operand, right_operand, preferred_element_type=jnp.float32
        )

    real_part = pairwise(green_real, green_real) + pairwise(green_imag, green_imag)
    imag_part = pairwise(green_real, green_imag) - pairwise(green_imag, green_real)
    partial_corr = jnp.stack([real_part, imag_part], axis=0) / receivers
    correlation = lax.psum_scatter(
        partial_corr.astype(jnp.bfloat16), "rcv", scatter_dimension=2, tiled=True
    ).astype(jnp.float32)
    return (focus_plus, focus_minus, correlation)


CHUNKS = 2
GROUP = 4
PIECES = 2
MESH = pl.DeviceIdType.MESH


def kernel(
    n, direct, onset, fwd, inv, refl, fp, fm, corr,
    ref_t, stage, zs, zr, ys, yr, rs, rr, own, minus, green, rows, edges, cs, cr,
    load_sem, z_send, z_recv, y_send, y_recv, r_send, r_recv, c_send, c_recv,
):
    me = lax.axis_index("freq")
    side = lax.axis_index("rcv")
    other = 1 - side
    traces, points, samples = direct.shape
    width = points // CHUNKS
    lanes = 2 * width
    bins, receivers, _ = ref_t.shape
    sources = receivers // 2
    freqs = n * bins
    groups = traces // GROUP
    f32, bf16 = jnp.float32, jnp.bfloat16

    barrier = pltpu.get_barrier_semaphore()

    def greet(k, carry):
        pl.semaphore_signal(
            barrier, inc=1, device_id=(lax.rem(me + k, n), side), device_id_type=MESH
        )
        return carry

    lax.fori_loop(1, n, greet, 0)
    pl.semaphore_signal(barrier, inc=1, device_id=(me, other), device_id_type=MESH)

    def load(f):
        slot = lax.rem(f, 2)
        return pltpu.make_async_copy(refl.at[:, f], stage.at[slot], load_sem.at[slot])

    load(0).start()
    load(1).start()

    def exchange(src, dst, send, recv, k):
        off = k + 1
        peer = lax.rem(me + off, n)
        return pltpu.make_async_remote_copy(
            src_ref=src.at[peer],
            dst_ref=dst.at[me],
            send_sem=send.at[off],
            recv_sem=recv.at[off],
            device_id=(peer, side),
            device_id_type=MESH,
        )

    def arrival(src, dst, send, recv, off):
        giver = lax.rem(me - off + n, n)
        return pltpu.make_async_remote_copy(
            src_ref=src.at[giver],
            dst_ref=dst.at[giver],
            send_sem=send.at[off],
            recv_sem=recv.at[off],
            device_id=(giver, side),
            device_id_type=MESH,
        )

    def send_all(ops):
        def step(k, carry):
            exchange(*ops, k).start()
            return carry

        lax.fori_loop(0, n - 1, step, 0)
        src, dst = ops[0], ops[1]
        dst[me] = src[me]

    def wait_all(ops):
        def step(off, carry):
            arrival(*ops, off).wait_recv()
            return carry

        lax.fori_loop(1, n, step, 0)

    def drain_all(ops):
        def step(off, carry):
            arrival(*ops, off).wait_send()
            return carry

        lax.fori_loop(1, n, step, 0)

    def z_ops(p, c):
        return zs.at[p, c], zr.at[p, c], z_send.at[p, c], z_recv.at[p, c]

    def y_ops(p, c, h):
        return ys.at[p, c, h], yr.at[p, c, h], y_send.at[p, c, h], y_recv.at[p, c, h]

    def half_copy(p, c, f):
        return pltpu.make_async_remote_copy(
            src_ref=rs.at[p, c, f],
            dst_ref=rr.at[p, c, f],
            send_sem=r_send.at[p, c, f],
            recv_sem=r_recv.at[p, c, f],
            device_id=(me, other),
            device_id_type=MESH,
        )

    def corr_copy(f):
        return pltpu.make_async_remote_copy(
            src_ref=cs.at[other, f],
            dst_ref=cr.at[f],
            send_sem=c_send.at[f],
            recv_sem=c_recv.at[f],
            device_id=(me, other),
            device_id_type=MESH,
        )

    def to_spectrum(p, c, g, block):
        spec = jnp.dot(block, fwd[...], preferred_element_type=f32)
        for u in range(GROUP):
            a = spec[u * width : (u + 1) * width]
            turned = jnp.concatenate([a[:, :freqs], a[:, freqs:]], axis=0).T
            zs[p, c, :, g * GROUP + u] = turned.reshape(n, bins, lanes).astype(bf16)

    def first(c):
        def step(g, carry):
            block = direct[pl.ds(g * GROUP, GROUP), c * width : (c + 1) * width, :]
            to_spectrum(0, c, g, block.reshape(GROUP * width, samples))
            return carry

        lax.fori_loop(0, groups, step, 0)

    def unpack(src, offset, size, stride):
        def step(j, carry):
            rows[pl.ds(pl.multiple_of(offset + j * stride, size), size), :] = (
                src[j].astype(f32).reshape(size, lanes)
            )
            return carry

        lax.fori_loop(0, n, step, 0)

    def back(p, c):
        whole = traces * bins
        piece = whole // PIECES
        for h in range(PIECES):
            wait_all(y_ops(p, c, h))
            unpack(yr.at[p, c, h], h * piece, piece, whole)
        cols = slice(c * width, (c + 1) * width)

        def step(g, carry):
            parts = []
            for u in range(GROUP):
                t = rows[pl.ds(g * GROUP + u, freqs, stride=traces), :].T
                parts.append(jnp.concatenate([t[:width], t[width:]], axis=1))
            lhs = jnp.concatenate(parts, axis=0).astype(bf16)
            out = jnp.dot(lhs, inv[...], preferred_element_type=f32)
            size = GROUP * width
            edge = edges[c, pl.ds(pl.multiple_of(g * size, size), size), :]
            edge = jnp.concatenate([edge] * (samples // points), axis=1)
            sample = lax.broadcasted_iota(jnp.int32, out.shape, 1).astype(f32)
            out = jnp.where(sample < edge, out, 0.0)
            at = pl.ds(g * GROUP, GROUP)
            if p == 0:
                block = out.astype(bf16)
                fm[at, cols, :] = block.reshape(GROUP, width, samples)
            else:
                old = direct[at, cols, :].astype(f32).reshape(size, samples)
                block = (old + out).astype(bf16)
                fp[at, cols, :] = block.reshape(GROUP, width, samples)
            to_spectrum(p + 1, c, g, block)
            return carry

        lax.fori_loop(0, groups, step, 0)
        send_all(z_ops(p + 1, c))

    def apply(p, c, sign):
        wait_all(z_ops(p, c))
        unpack(zr.at[p, c], 0, traces * bins, traces * bins)

        def step(f, carry):
            x = rows[pl.ds(f, sources, stride=bins), :]
            if p == 1:
                minus[c, f] = x.astype(bf16)
            y = pltpu.roll(x, width, 1)
            low = lax.broadcasted_iota(jnp.int32, x.shape, 1) < width
            y = jnp.where(low, -y, y) if sign > 0 else jnp.where(low, y, -y)
            w = jnp.concatenate([x.astype(bf16), y.astype(bf16)], axis=0)
            theirs = ref_t[f, pl.ds(pl.multiple_of(other * sources, sources), sources), :]
            rs[p, c, f] = jnp.dot(theirs, w, preferred_element_type=f32).astype(bf16)
            half_copy(p, c, f).start()
            mine = ref_t[f, pl.ds(pl.multiple_of(side * sources, sources), sources), :]
            own[c, f] = jnp.dot(mine, w, preferred_element_type=f32).astype(bf16)
            return carry

        lax.fori_loop(0, bins, step, 0)

    def reduce(p, c):
        part = bins // PIECES
        for h in range(PIECES):

            def step(k, carry):
                f = h * part + k
                half_copy(p, c, f).wait_recv()
                total = own[c, f].astype(f32) + rr[p, c, f].astype(f32)
                if p < 2:
                    ys[p, c, h, :, k] = total.reshape(n, traces, lanes).astype(bf16)
                else:
                    green[c, f] = (total - minus[c, f].astype(f32)).astype(bf16)
                return carry

            lax.fori_loop(0, part, step, 0)
            if p < 2:
                send_all(y_ops(p, c, h))

    def transpose(f, carry):
        load(f).wait()
        slot = lax.rem(f, 2)
        for c in range(2):
            ref_t[f, :, c * sources : (c + 1) * sources] = stage[slot, c].T

        @pl.when(f + 2 < bins)
        def _():
            load(f + 2).start()

        return carry

    def columns(s, carry):
        row = onset[pl.ds(s, 1), :].astype(f32)
        turned = jnp.broadcast_to(row, (points, points)).T
        for c in range(CHUNKS):
            at = pl.ds(pl.multiple_of(s * width, width), width)
            edges[c, at, :] = turned[c * width : (c + 1) * width]
        return carry

    first(0)
    pl.semaphore_wait(barrier, n)
    send_all(z_ops(0, 0))
    first(1)
    lax.fori_loop(0, traces, columns, 0)
    lax.fori_loop(0, bins, transpose, 0)
    drain_all(z_ops(0, 0))
    send_all(z_ops(0, 1))
    apply(0, 0, 1)
    reduce(0, 0)
    apply(0, 1, 1)
    reduce(0, 1)
    back(0, 0)
    back(0, 1)
    apply(1, 0, -1)
    reduce(1, 0)
    apply(1, 1, -1)
    reduce(1, 1)
    back(1, 0)
    back(1, 1)
    apply(2, 0, 1)
    reduce(2, 0)
    apply(2, 1, 1)
    reduce(2, 1)

    half = points // 2

    def correlate(f, carry):
        a, b = green[0, f].astype(f32), green[1, f].astype(f32)
        low = lax.broadcasted_iota(jnp.int32, a.shape, 1) < width
        real = jnp.where(low, a, pltpu.roll(b, width, 1))
        imag = jnp.where(low, pltpu.roll(a, width, 1), b)
        both = jnp.concatenate([real, imag], axis=1).astype(bf16)
        prod = lax.dot_general(
            both, both, (((0,), (0,)), ((), ())), preferred_element_type=f32
        )
        re = (prod[:points, :points] + prod[points:, points:]) / receivers
        im = (prod[:points, points:] - prod[points:, :points]) / receivers
        for h in range(2):
            cs[h, f, 0] = re[h * half : (h + 1) * half].astype(bf16)
            cs[h, f, 1] = im[h * half : (h + 1) * half].astype(bf16)
        corr_copy(f).start()
        return carry

    lax.fori_loop(0, bins, correlate, 0)

    def collect(f, carry):
        corr_copy(f).wait_recv()
        for c in range(2):
            corr[c, f] = cs[side, f, c].astype(f32) + cr[f, c].astype(f32)
        return carry

    lax.fori_loop(0, bins, collect, 0)

    for c in range(CHUNKS):
        for p in range(3):
            if (p, c) != (0, 0):
                drain_all(z_ops(p, c))

            def drain(f, carry):
                half_copy(p, c, f).wait_send()
                return carry

            lax.fori_loop(0, bins, drain, 0)
        for p in range(2):
            for h in range(PIECES):
                drain_all(y_ops(p, c, h))

    def drain_corr(f, carry):
        corr_copy(f).wait_send()
        return carry

    lax.fori_loop(0, bins, drain_corr, 0)


def fused(reflection, direct, onset):
    n = lax.axis_size("freq")
    traces, points, samples = direct.shape
    _, bins, sources, receivers = reflection.shape
    width = points // CHUNKS
    frequencies = bins * n
    phase = np.arange(samples)[:, None] * np.arange(frequencies)[None, :] % samples
    angles = np.float32(2.0 * math.pi / samples) * phase.astype(np.float32)
    waves = np.concatenate([np.cos(angles), -np.sin(angles)], axis=1)
    forward = (waves / np.float32(math.sqrt(samples))).astype(jnp.bfloat16)
    inverse = (waves.T * np.float32(2.0 / math.sqrt(samples))).astype(jnp.bfloat16)
    bf16, dma = jnp.bfloat16, pltpu.SemaphoreType.DMA
    lanes = 2 * width
    vmem = pl.BlockSpec(memory_space=pltpu.VMEM)
    return pl.pallas_call(
        functools.partial(kernel, n),
        out_shape=(
            jax.ShapeDtypeStruct(direct.shape, bf16),
            jax.ShapeDtypeStruct(direct.shape, bf16),
            jax.ShapeDtypeStruct((2, bins, points // 2, points), jnp.float32),
        ),
        in_specs=[vmem, vmem, vmem, vmem, pl.BlockSpec(memory_space=pl.ANY)],
        out_specs=(vmem, vmem, vmem),
        scratch_shapes=[
            pltpu.VMEM((bins, receivers, 2 * sources), bf16),
            pltpu.VMEM((2, 2, sources, receivers), bf16),
            pltpu.VMEM((3, CHUNKS, n, traces, bins, lanes), bf16),
            pltpu.VMEM((3, CHUNKS, n, traces, bins, lanes), bf16),
            pltpu.VMEM((2, CHUNKS, PIECES, n, bins // PIECES, traces, lanes), bf16),
            pltpu.VMEM((2, CHUNKS, PIECES, n, bins // PIECES, traces, lanes), bf16),
            pltpu.VMEM((3, CHUNKS, bins, sources, lanes), bf16),
            pltpu.VMEM((3, CHUNKS, bins, sources, lanes), bf16),
            pltpu.VMEM((CHUNKS, bins, sources, lanes), bf16),
            pltpu.VMEM((CHUNKS, bins, sources, lanes), bf16),
            pltpu.VMEM((CHUNKS, bins, sources, lanes), bf16),
            pltpu.VMEM((n * traces * bins, lanes), jnp.float32),
            pltpu.VMEM((CHUNKS, traces * width, points), jnp.float32),
            pltpu.VMEM((2, bins, 2, points // 2, points), bf16),
            pltpu.VMEM((bins, 2, points // 2, points), bf16),
            dma((2,)),
            dma((3, CHUNKS, n)),
            dma((3, CHUNKS, n)),
            dma((2, CHUNKS, PIECES, n)),
            dma((2, CHUNKS, PIECES, n)),
            dma((3, CHUNKS, bins)),
            dma((3, CHUNKS, bins)),
            dma((bins,)),
            dma((bins,)),
        ],
        compiler_params=pltpu.CompilerParams(
            collective_id=0, has_side_effects=True, vmem_limit_bytes=67043328
        ),
    )(direct, onset, jnp.asarray(forward), jnp.asarray(inverse), reflection)


def fits(reflection, direct):
    n = lax.axis_size("freq")
    traces, points, samples = direct.shape
    _, bins, sources, receivers = reflection.shape
    return (
        lax.axis_size("rcv") == 2
        and receivers == 2 * sources
        and sources == n * traces
        and traces % 8 == 0
        and bins % 8 == 0
        and points == 128
        and samples % 128 == 0
        and (bins * n) % 128 == 0
    )


def per_device(reflection, direct, onset):
    if fits(reflection, direct):
        return fused(reflection, direct, onset)
    return on_device(reflection, direct, onset)


def solution(mesh):
    placed = (
        P(None, "freq", "rcv", None),
        P(("rcv", "freq"), None, None),
        P(("rcv", "freq"), None),
    )
    return jax.shard_map(
        per_device,
        mesh=mesh,
        in_specs=placed,
        out_specs=(
            P(("rcv", "freq"), None, None),
            P(("rcv", "freq"), None, None),
            P(None, "freq", "rcv", None),
        ),
        check_vma=False,
    )
```

```python
import functools
import math

import jax
import jax.numpy as jnp
import numpy as np
from jax import lax
from jax.experimental import pallas as pl
from jax.experimental.pallas import tpu as pltpu
from jax.sharding import PartitionSpec as P


def lookup_tables(samples, frequencies):
    sample = jnp.arange(samples, dtype=jnp.int32)
    spectral_bin_index = jnp.arange(frequencies, dtype=jnp.int32)
    phase_index = sample[:, None] * spectral_bin_index[None, :] % samples
    angles = 2.0 * math.pi / samples * phase_index.astype(jnp.float32)
    cosine = jnp.cos(angles)
    sine = jnp.sin(angles)
    forward = (jnp.stack([cosine, -sine], axis=1) / math.sqrt(samples)).astype(jnp.bfloat16)
    inverse = (jnp.stack([cosine.T, -sine.T], axis=0) * (2.0 / math.sqrt(samples))).astype(
        jnp.bfloat16
    )
    return (forward, inverse)


def fourier_spectrum(field, forward):
    local_spectra = jnp.einsum(
        "sqt,tcf->scfq", field, forward, preferred_element_type=jnp.float32
    ).astype(jnp.bfloat16)
    return lax.all_to_all(local_spectra, "freq", split_axis=2, concat_axis=0, tiled=True)


def make_term(spectra, reflection, conj_sign):
    spectrum_real_rows = spectra[:, 0]
    spec_imag = spectra[:, 1]

    def product(left_operand, right_operand):
        return jnp.einsum(
            "key,ekn->ykn", left_operand, right_operand, preferred_element_type=jnp.float32
        )

    real_part = product(reflection[0], spectrum_real_rows) - conj_sign * product(
        reflection[1], spec_imag
    )
    imag_part = product(reflection[0], spec_imag) + conj_sign * product(
        reflection[1], spectrum_real_rows
    )
    return jnp.stack([real_part, imag_part], axis=1)


def to_time(spectra, reflection, conj_sign):
    summed = lax.psum_scatter(
        make_term(spectra, reflection, conj_sign).astype(jnp.bfloat16),
        "rcv",
        scatter_dimension=0,
        tiled=True,
    )
    return lax.all_to_all(summed, "freq", split_axis=0, concat_axis=2, tiled=True)


def inverse_window(summed, onset, inverse):
    traces = jnp.einsum("scfq,cft->sqt", summed, inverse, preferred_element_type=jnp.float32)
    sample = jnp.arange(traces.shape[2], dtype=jnp.int32)
    window = (sample[None, None, :] < onset[:, :, None]).astype(jnp.float32)
    return traces * window


def on_device(reflection, direct, onset):
    samples = direct.shape[2]
    frequencies = reflection.shape[1] * lax.axis_size("freq")
    forward, inverse = lookup_tables(samples, frequencies)
    focus_plus = direct
    minus_spectrum = None
    plus_spectrum = fourier_spectrum(focus_plus, forward)
    focus_minus = inverse_window(to_time(plus_spectrum, reflection, 1.0), onset, inverse).astype(
        jnp.bfloat16
    )
    minus_spectrum = fourier_spectrum(focus_minus, forward)
    returned = inverse_window(to_time(minus_spectrum, reflection, -1.0), onset, inverse)
    focus_plus = (direct.astype(jnp.float32) + returned).astype(jnp.bfloat16)
    plus_spectrum = fourier_spectrum(focus_plus, forward)
    receivers = reflection.shape[3]
    summed = lax.psum_scatter(
        make_term(plus_spectrum, reflection, 1.0).astype(jnp.bfloat16),
        "rcv",
        scatter_dimension=0,
        tiled=True,
    ).astype(jnp.float32)
    green_field = (summed - minus_spectrum.astype(jnp.float32)).astype(jnp.bfloat16)
    green_real = green_field[:, 0]
    green_imag = green_field[:, 1]

    def pairwise(left_operand, right_operand):
        return jnp.einsum(
            "rfa,rfb->fab", left_operand, right_operand, preferred_element_type=jnp.float32
        )

    real_part = pairwise(green_real, green_real) + pairwise(green_imag, green_imag)
    imag_part = pairwise(green_real, green_imag) - pairwise(green_imag, green_real)
    partial_corr = jnp.stack([real_part, imag_part], axis=0) / receivers
    correlation = lax.psum_scatter(
        partial_corr.astype(jnp.bfloat16), "rcv", scatter_dimension=2, tiled=True
    ).astype(jnp.float32)
    return (focus_plus, focus_minus, correlation)


CHUNKS = 2
GROUP = 4
PIECES = 2
MESH = pl.DeviceIdType.MESH


def kernel(
    n, direct, onset, fwd, inv, refl, fp, fm, corr,
    ref_t, stage, zs, zr, ys, yr, rs, rr, own, minus, green, rows, edges, cs, cr,
    load_sem, z_send, z_recv, y_send, y_recv, r_send, r_recv, c_send, c_recv,
):
    me = lax.axis_index("freq")
    side = lax.axis_index("rcv")
    other = 1 - side
    traces, points, samples = direct.shape
    width = points // CHUNKS
    lanes = 2 * width
    bins, receivers, _ = ref_t.shape
    sources = receivers // 2
    freqs = n * bins
    groups = traces // GROUP
    f32, bf16 = jnp.float32, jnp.bfloat16

    barrier = pltpu.get_barrier_semaphore()

    def greet(k, carry):
        pl.semaphore_signal(
            barrier, inc=1, device_id=(lax.rem(me + k, n), side), device_id_type=MESH
        )
        return carry

    lax.fori_loop(1, n, greet, 0)
    pl.semaphore_signal(barrier, inc=1, device_id=(me, other), device_id_type=MESH)

    def load(f):
        slot = lax.rem(f, 2)
        return pltpu.make_async_copy(refl.at[:, f], stage.at[slot], load_sem.at[slot])

    load(0).start()
    load(1).start()

    def exchange(src, dst, send, recv, k):
        off = k + 1
        peer = lax.rem(me + off, n)
        return pltpu.make_async_remote_copy(
            src_ref=src.at[peer],
            dst_ref=dst.at[me],
            send_sem=send.at[off],
            recv_sem=recv.at[off],
            device_id=(peer, side),
            device_id_type=MESH,
        )

    def arrival(src, dst, send, recv, off):
        giver = lax.rem(me - off + n, n)
        return pltpu.make_async_remote_copy(
            src_ref=src.at[giver],
            dst_ref=dst.at[giver],
            send_sem=send.at[off],
            recv_sem=recv.at[off],
            device_id=(giver, side),
            device_id_type=MESH,
        )

    def send_all(ops):
        def step(k, carry):
            exchange(*ops, k).start()
            return carry

        lax.fori_loop(0, n - 1, step, 0)
        src, dst = ops[0], ops[1]
        dst[me] = src[me]

    def wait_all(ops):
        def step(off, carry):
            arrival(*ops, off).wait_recv()
            return carry

        lax.fori_loop(1, n, step, 0)

    def drain_all(ops):
        def step(off, carry):
            arrival(*ops, off).wait_send()
            return carry

        lax.fori_loop(1, n, step, 0)

    def z_ops(p, c):
        return zs.at[p, c], zr.at[p, c], z_send.at[p, c], z_recv.at[p, c]

    def y_ops(p, c, h):
        return ys.at[p, c, h], yr.at[p, c, h], y_send.at[p, c, h], y_recv.at[p, c, h]

    def half_copy(p, c, f):
        return pltpu.make_async_remote_copy(
            src_ref=rs.at[p, c, f],
            dst_ref=rr.at[p, c, f],
            send_sem=r_send.at[p, c, f],
            recv_sem=r_recv.at[p, c, f],
            device_id=(me, other),
            device_id_type=MESH,
        )

    def corr_copy(f):
        return pltpu.make_async_remote_copy(
            src_ref=cs.at[other, f],
            dst_ref=cr.at[f],
            send_sem=c_send.at[f],
            recv_sem=c_recv.at[f],
            device_id=(me, other),
            device_id_type=MESH,
        )

    def to_spectrum(p, c, g, block):
        spec = jnp.dot(block, fwd[...], preferred_element_type=f32)
        for u in range(GROUP):
            a = spec[u * width : (u + 1) * width]
            turned = jnp.concatenate([a[:, :freqs], a[:, freqs:]], axis=0).T
            zs[p, c, :, g * GROUP + u] = turned.reshape(n, bins, lanes).astype(bf16)

    def first(c):
        def step(g, carry):
            block = direct[pl.ds(g * GROUP, GROUP), c * width : (c + 1) * width, :]
            to_spectrum(0, c, g, block.reshape(GROUP * width, samples))
            return carry

        lax.fori_loop(0, groups, step, 0)

    def unpack(src, offset, size, stride):
        def step(j, carry):
            rows[pl.ds(pl.multiple_of(offset + j * stride, size), size), :] = (
                src[j].astype(f32).reshape(size, lanes)
            )
            return carry

        lax.fori_loop(0, n, step, 0)

    def back(p, c):
        whole = traces * bins
        piece = whole // PIECES
        for h in range(PIECES):
            wait_all(y_ops(p, c, h))
            unpack(yr.at[p, c, h], h * piece, piece, whole)
        cols = slice(c * width, (c + 1) * width)

        def step(g, carry):
            parts = []
            for u in range(GROUP):
                t = rows[pl.ds(g * GROUP + u, freqs, stride=traces), :].T
                parts.append(jnp.concatenate([t[:width], t[width:]], axis=1))
            lhs = jnp.concatenate(parts, axis=0).astype(bf16)
            out = jnp.dot(lhs, inv[...], preferred_element_type=f32)
            size = GROUP * width
            edge = edges[c, pl.ds(pl.multiple_of(g * size, size), size), :]
            edge = jnp.concatenate([edge] * (samples // points), axis=1)
            sample = lax.broadcasted_iota(jnp.int32, out.shape, 1).astype(f32)
            out = jnp.where(sample < edge, out, 0.0)
            at = pl.ds(g * GROUP, GROUP)
            if p == 0:
                block = out.astype(bf16)
                fm[at, cols, :] = block.reshape(GROUP, width, samples)
            else:
                old = direct[at, cols, :].astype(f32).reshape(size, samples)
                block = (old + out).astype(bf16)
                fp[at, cols, :] = block.reshape(GROUP, width, samples)
            to_spectrum(p + 1, c, g, block)
            return carry

        lax.fori_loop(0, groups, step, 0)
        send_all(z_ops(p + 1, c))

    def apply(p, c, sign):
        wait_all(z_ops(p, c))
        unpack(zr.at[p, c], 0, traces * bins, traces * bins)

        def step(f, carry):
            x = rows[pl.ds(f, sources, stride=bins), :]
            if p == 1:
                minus[c, f] = x.astype(bf16)
            y = pltpu.roll(x, width, 1)
            low = lax.broadcasted_iota(jnp.int32, x.shape, 1) < width
            y = jnp.where(low, -y, y) if sign > 0 else jnp.where(low, y, -y)
            w = jnp.concatenate([x.astype(bf16), y.astype(bf16)], axis=0)
            theirs = ref_t[f, pl.ds(pl.multiple_of(other * sources, sources), sources), :]
            rs[p, c, f] = jnp.dot(theirs, w, preferred_element_type=f32).astype(bf16)
            half_copy(p, c, f).start()
            mine = ref_t[f, pl.ds(pl.multiple_of(side * sources, sources), sources), :]
            own[c, f] = jnp.dot(mine, w, preferred_element_type=f32).astype(bf16)
            return carry

        lax.fori_loop(0, bins, step, 0)

    def reduce(p, c, pieces=range(PIECES)):
        part = bins // PIECES
        for h in pieces:

            def step(k, carry):
                f = h * part + k
                half_copy(p, c, f).wait_recv()
                total = own[c, f].astype(f32) + rr[p, c, f].astype(f32)
                if p < 2:
                    ys[p, c, h, :, k] = total.reshape(n, traces, lanes).astype(bf16)
                else:
                    green[c, f] = (total - minus[c, f].astype(f32)).astype(bf16)
                return carry

            lax.fori_loop(0, part, step, 0)
            if p < 2:
                send_all(y_ops(p, c, h))

    def transpose(f, carry):
        load(f).wait()
        slot = lax.rem(f, 2)
        for c in range(2):
            ref_t[f, :, c * sources : (c + 1) * sources] = stage[slot, c].T

        @pl.when(f + 2 < bins)
        def _():
            load(f + 2).start()

        return carry

    def columns(s, carry):
        row = onset[pl.ds(s, 1), :].astype(f32)
        turned = jnp.broadcast_to(row, (points, points)).T
        for c in range(CHUNKS):
            at = pl.ds(pl.multiple_of(s * width, width), width)
            edges[c, at, :] = turned[c * width : (c + 1) * width]
        return carry

    first(0)
    pl.semaphore_wait(barrier, n)
    send_all(z_ops(0, 0))
    first(1)
    lax.fori_loop(0, traces, columns, 0)
    lax.fori_loop(0, bins, transpose, 0)
    drain_all(z_ops(0, 0))
    send_all(z_ops(0, 1))
    apply(0, 0, 1)
    reduce(0, 0, range(PIECES - 1))
    apply(0, 1, 1)
    reduce(0, 0, range(PIECES - 1, PIECES))
    reduce(0, 1)
    back(0, 0)
    back(0, 1)
    apply(1, 0, -1)
    reduce(1, 0, range(PIECES - 1))
    apply(1, 1, -1)
    reduce(1, 0, range(PIECES - 1, PIECES))
    reduce(1, 1)
    back(1, 0)
    back(1, 1)
    apply(2, 0, 1)
    apply(2, 1, 1)
    reduce(2, 0)
    reduce(2, 1)

    half = points // 2

    def correlate(f, carry):
        a, b = green[0, f].astype(f32), green[1, f].astype(f32)
        low = lax.broadcasted_iota(jnp.int32, a.shape, 1) < width
        real = jnp.where(low, a, pltpu.roll(b, width, 1))
        imag = jnp.where(low, pltpu.roll(a, width, 1), b)
        both = jnp.concatenate([real, imag], axis=1).astype(bf16)
        prod = lax.dot_general(
            both, both, (((0,), (0,)), ((), ())), preferred_element_type=f32
        )
        re = (prod[:points, :points] + prod[points:, points:]) / receivers
        im = (prod[:points, points:] - prod[points:, :points]) / receivers
        for h in range(2):
            cs[h, f, 0] = re[h * half : (h + 1) * half].astype(bf16)
            cs[h, f, 1] = im[h * half : (h + 1) * half].astype(bf16)
        corr_copy(f).start()
        return carry

    lax.fori_loop(0, bins, correlate, 0)

    def collect(f, carry):
        corr_copy(f).wait_recv()
        for c in range(2):
            corr[c, f] = cs[side, f, c].astype(f32) + cr[f, c].astype(f32)
        return carry

    lax.fori_loop(0, bins, collect, 0)

    for c in range(CHUNKS):
        for p in range(3):
            if (p, c) != (0, 0):
                drain_all(z_ops(p, c))

            def drain(f, carry):
                half_copy(p, c, f).wait_send()
                return carry

            lax.fori_loop(0, bins, drain, 0)
        for p in range(2):
            for h in range(PIECES):
                drain_all(y_ops(p, c, h))

    def drain_corr(f, carry):
        corr_copy(f).wait_send()
        return carry

    lax.fori_loop(0, bins, drain_corr, 0)


def fused(reflection, direct, onset):
    n = lax.axis_size("freq")
    traces, points, samples = direct.shape
    _, bins, sources, receivers = reflection.shape
    width = points // CHUNKS
    frequencies = bins * n
    phase = np.arange(samples)[:, None] * np.arange(frequencies)[None, :] % samples
    angles = np.float32(2.0 * math.pi / samples) * phase.astype(np.float32)
    waves = np.concatenate([np.cos(angles), -np.sin(angles)], axis=1)
    forward = (waves / np.float32(math.sqrt(samples))).astype(jnp.bfloat16)
    inverse = (waves.T * np.float32(2.0 / math.sqrt(samples))).astype(jnp.bfloat16)
    bf16, dma = jnp.bfloat16, pltpu.SemaphoreType.DMA
    lanes = 2 * width
    vmem = pl.BlockSpec(memory_space=pltpu.VMEM)
    return pl.pallas_call(
        functools.partial(kernel, n),
        out_shape=(
            jax.ShapeDtypeStruct(direct.shape, bf16),
            jax.ShapeDtypeStruct(direct.shape, bf16),
            jax.ShapeDtypeStruct((2, bins, points // 2, points), jnp.float32),
        ),
        in_specs=[vmem, vmem, vmem, vmem, pl.BlockSpec(memory_space=pl.ANY)],
        out_specs=(vmem, vmem, vmem),
        scratch_shapes=[
            pltpu.VMEM((bins, receivers, 2 * sources), bf16),
            pltpu.VMEM((2, 2, sources, receivers), bf16),
            pltpu.VMEM((3, CHUNKS, n, traces, bins, lanes), bf16),
            pltpu.VMEM((3, CHUNKS, n, traces, bins, lanes), bf16),
            pltpu.VMEM((2, CHUNKS, PIECES, n, bins // PIECES, traces, lanes), bf16),
            pltpu.VMEM((2, CHUNKS, PIECES, n, bins // PIECES, traces, lanes), bf16),
            pltpu.VMEM((3, CHUNKS, bins, sources, lanes), bf16),
            pltpu.VMEM((3, CHUNKS, bins, sources, lanes), bf16),
            pltpu.VMEM((CHUNKS, bins, sources, lanes), bf16),
            pltpu.VMEM((CHUNKS, bins, sources, lanes), bf16),
            pltpu.VMEM((CHUNKS, bins, sources, lanes), bf16),
            pltpu.VMEM((n * traces * bins, lanes), jnp.float32),
            pltpu.VMEM((CHUNKS, traces * width, points), jnp.float32),
            pltpu.VMEM((2, bins, 2, points // 2, points), bf16),
            pltpu.VMEM((bins, 2, points // 2, points), bf16),
            dma((2,)),
            dma((3, CHUNKS, n)),
            dma((3, CHUNKS, n)),
            dma((2, CHUNKS, PIECES, n)),
            dma((2, CHUNKS, PIECES, n)),
            dma((3, CHUNKS, bins)),
            dma((3, CHUNKS, bins)),
            dma((bins,)),
            dma((bins,)),
        ],
        compiler_params=pltpu.CompilerParams(
            collective_id=0, has_side_effects=True, vmem_limit_bytes=67043328
        ),
    )(direct, onset, jnp.asarray(forward), jnp.asarray(inverse), reflection)


def fits(reflection, direct):
    n = lax.axis_size("freq")
    traces, points, samples = direct.shape
    _, bins, sources, receivers = reflection.shape
    return (
        lax.axis_size("rcv") == 2
        and receivers == 2 * sources
        and sources == n * traces
        and traces % 8 == 0
        and bins % 8 == 0
        and points == 128
        and samples % 128 == 0
        and (bins * n) % 128 == 0
    )


def per_device(reflection, direct, onset):
    if fits(reflection, direct):
        return fused(reflection, direct, onset)
    return on_device(reflection, direct, onset)


def solution(mesh):
    placed = (
        P(None, "freq", "rcv", None),
        P(("rcv", "freq"), None, None),
        P(("rcv", "freq"), None),
    )
    return jax.shard_map(
        per_device,
        mesh=mesh,
        in_specs=placed,
        out_specs=(
            P(("rcv", "freq"), None, None),
            P(("rcv", "freq"), None, None),
            P(None, "freq", "rcv", None),
        ),
        check_vma=False,
    )
```
